128 devices in a mesh: dp: 16 (over z_hi, x, core), group: 8 (over y, z_lo).
Axes of the slice: x: 4, y: 4, z: 4 (z_hi: 2, z_lo: 2; z = z_hi * 2 + z_lo), core: 2. Of those that a mesh axis runs over, the one named last changes fastest.
Arguments:
- volume: bfloat16 [256, 256, 2, 256], P('group'), may hold values from -6 to 6
- images: bfloat16 [2048, 256, 256], P(('dp', 'group')), may hold values from -6 to 6
- orientation: int32 [32], replicated, may hold values from 0 to 359
- batch_slot: int32 [2048], P(('dp', 'group')), may hold values from 0 to 1
- ctf_class: int32 [2048], P(('dp', 'group')), may hold values from 0 to 15
Outputs:
- grad_volume: float32 [256, 256, 2, 256], P('group', 'dp')
The draws below stay inside these ranges and needn't reach their ends.
All inputs are finite; a program needn't handle non-finite values.
Results may differ from the reference program's by a relative error of at most 0.0095.
Values may be sent and summed in bfloat16 or wider, within the bound.
A program may use at most 128 MiB of HBM per device.

```python
import jax
import jax.numpy as jnp
from jax import lax

L = 256
NROT = 360
NCTF = 16
ORI_DEV = 2
NBATCH = 16
BATCH_PARTS = 128
ORIENTS = 32
PARTICLES = 2048


def with_ends(entries, stream_key, least, high):
    shape = entries.shape
    index_at = [jax.random.randint(jax.random.fold_in(stream_key, axis), (), 0, shape[axis]) for axis in range(len(shape))]
    entries = entries.at[tuple(index_at)].set(least)
    longest = shape.index(max(shape))
    index_at[longest] = (index_at[longest] + 1) % shape[longest]
    return entries.at[tuple(index_at)].set(high)


def block_levels(key, dims, shards, low, high):
    level = 1.0
    for position, shards_of in shards:
        heights = jax.random.uniform(jax.random.fold_in(jax.random.fold_in(key, 6), position), (shards_of,), jnp.float32, low / len(shards), high / len(shards))
        level = level * jnp.repeat(jnp.exp(heights), dims[position] // shards_of).reshape((-1,) + (1,) * (len(dims) - 1 - position))
    return level


def gaussian(own_key, dims, width, limit, cuts=(), held_as=jnp.bfloat16):
    gain = block_levels(own_key, dims, cuts, -0.22, 0.18) if cuts else 1.0
    values = jax.random.normal(own_key, dims, jnp.float32) * width * gain
    return jnp.minimum(jnp.maximum(values, -limit), limit).astype(held_as)


def setup_inputs(seed: int = 0) -> dict:
    arg_keys = jax.random.split(jax.random.key(seed), 6)
    return {
        "volume": gaussian(arg_keys[0], (L, L, 2, L), 1.0, 6.0, ((0, 8),)),
        "images": gaussian(arg_keys[1], (PARTICLES, L, L), 1.0, 6.0, ((0, 128),)),
        "orientation": with_ends(jax.random.randint(arg_keys[2], (ORIENTS,), 0, NROT), jax.random.fold_in(arg_keys[2], 1), 0, NROT - 1).astype(jnp.int32),
        "batch_slot": with_ends(jax.random.randint(arg_keys[3], (PARTICLES,), 0, ORI_DEV), jax.random.fold_in(arg_keys[3], 1), 0, ORI_DEV - 1).astype(jnp.int32),
        "ctf_class": with_ends(jax.random.randint(arg_keys[4], (PARTICLES,), 0, NCTF), jax.random.fold_in(arg_keys[4], 1), 0, NCTF - 1).astype(jnp.int32),
    }


PRIOR_WEIGHT = 0.25


def neighbours(orient_ids, length):
    tilt_angle = jnp.pi * (orient_ids.astype(jnp.float32) + 0.5) / NROT
    offset = (jnp.arange(length, dtype=jnp.int32) - length // 2).astype(jnp.float32)
    coord_z = length / 2 + offset[None, :] * jnp.sin(tilt_angle)[:, None]
    coord_y = length / 2 + offset[None, :] * jnp.cos(tilt_angle)[:, None]
    floor_z = jnp.floor(coord_z)
    floor_y = jnp.floor(coord_y)
    frac_z = coord_z - floor_z
    frac_y = coord_y - floor_y
    base_z = floor_z.astype(jnp.int32)
    base_y = floor_y.astype(jnp.int32)
    corner_z, corner_y, corner_w = [], [], []
    for step_z in (0, 1):
        for step_y in (0, 1):
            corner_z.append(base_z + step_z)
            corner_y.append(base_y + step_y)
            part_z = frac_z if step_z else 1.0 - frac_z
            part_y = frac_y if step_y else 1.0 - frac_y
            corner_w.append(part_z * part_y)
    return jnp.stack(corner_z, axis=1), jnp.stack(corner_y, axis=1), jnp.stack(corner_w, axis=1)


def extract(planes, orient_ids, z_start, z_len, length):
    plane_z, plane_y, weight = neighbours(orient_ids, length)
    local_z = plane_z - z_start
    inside = (local_z >= 0) & (local_z < z_len) & (plane_y >= 0) & (plane_y < length)
    row_index = jnp.where(inside, local_z * length + plane_y, 0).astype(jnp.int32)
    weight = jnp.where(inside, weight, jnp.zeros_like(weight))
    picked = jnp.take(planes, row_index.reshape(-1), axis=0)
    picked = picked.reshape(orient_ids.shape[0], 4, length, 2, length)
    return jnp.sum(picked * weight[:, :, :, None, None], axis=1)


def backproject(summed, slice_grads, orient_ids, z_start, z_len, y_start, y_len):
    length = slice_grads.shape[-1]
    plane_z, plane_y, weight = neighbours(orient_ids, length)
    local_z = plane_z - z_start
    local_y = plane_y - y_start
    inside = (local_z >= 0) & (local_z < z_len) & (local_y >= 0) & (local_y < y_len)
    row_index = jnp.where(inside, local_z * y_len + local_y, 0).astype(jnp.int32)
    weight = jnp.where(inside, weight, jnp.zeros_like(weight))

    def add_slice(accum, items):
        grad_one, index_one, weight_one = items
        values = grad_one.astype(jnp.float32)[None] * weight_one[:, :, None, None]
        return accum.at[index_one.reshape(-1)].add(values.reshape(-1, 2, length)), None

    summed, unused = lax.scan(add_slice, summed, (slice_grads, row_index, weight))
    return summed


def contrast(classes, length):
    offset = (jnp.arange(length, dtype=jnp.int32) - length // 2).astype(jnp.float32)
    radius = (offset[:, None] ** 2 + offset[None, :] ** 2) / (length * length)
    defocus = 30.0 + 10.0 * classes.astype(jnp.float32)
    return -jnp.sin(defocus[:, None, None] * radius[None] + 0.1)


def reference(volume, images, orientation, batch_slot, ctf_class):
    length = volume.shape[-1]
    planes = volume.reshape(length * length, 2, length)
    orient_rows = orientation.reshape(NBATCH, ORI_DEV)
    image_rows = images.reshape(NBATCH, BATCH_PARTS, length, length)
    slot_rows = batch_slot.reshape(NBATCH, BATCH_PARTS)
    class_rows = ctf_class.reshape(NBATCH, BATCH_PARTS)

    def one_batch(items):
        orient_ids, pictures, slots, classes = items
        slices = extract(planes, orient_ids, 0, length, length)
        shifted = jnp.fft.fftshift(jnp.fft.fft2(pictures.astype(jnp.float32), norm="ortho"), axes=(-2, -1))
        spectrum = jnp.stack([jnp.real(shifted), jnp.imag(shifted)], axis=2)
        factor = contrast(classes, length)[:, :, None, :]
        predicted = jnp.take(slices, slots, axis=0)
        residual = factor * predicted - spectrum
        weighted = factor * residual
        onehot = (slots[:, None] == jnp.arange(ORI_DEV, dtype=jnp.int32)[None, :]).astype(jnp.float32)
        grads = jnp.einsum("ps,pjcx->sjcx", onehot, weighted, precision=lax.Precision.HIGHEST)
        return grads.astype(jnp.bfloat16)

    slice_grads = lax.map(one_batch, (orient_rows, image_rows, slot_rows, class_rows))
    slice_grads = slice_grads.reshape(ORIENTS, length, 2, length)
    summed = jnp.zeros((length * length, 2, length), jnp.float32)
    summed = backproject(summed, slice_grads, orientation, 0, length, 0, length)
    return summed.reshape(length, length, 2, length) + PRIOR_WEIGHT * volume.astype(jnp.float32)
```

```python
import math

import jax
import jax.numpy as jnp
from jax import lax
from jax.sharding import PartitionSpec as P

NROT = 360
ORI_DEV = 2


PRIOR_WEIGHT = 0.25


def axis_weights(base, frac, start, span):
    cells = jnp.arange(span, dtype=jnp.int32) + start
    lower = (cells[None, :, None] == base[:, None, :]).astype(jnp.float32) * (1.0 - frac)[
        :, None, :
    ]
    upper = (cells[None, :, None] == (base + 1)[:, None, :]).astype(jnp.float32) * frac[:, None, :]
    return lower + upper


def slice_matrix(orient_ids, length, z_start, z_len, y_start, y_len):
    tilt_angle = jnp.pi * (orient_ids.astype(jnp.float32) + 0.5) / NROT
    offset = (jnp.arange(length, dtype=jnp.int32) - length // 2).astype(jnp.float32)
    coord_z = length / 2 + offset[None, :] * jnp.sin(tilt_angle)[:, None]
    coord_y = length / 2 + offset[None, :] * jnp.cos(tilt_angle)[:, None]
    floor_z = jnp.floor(coord_z)
    floor_y = jnp.floor(coord_y)
    weight_z = axis_weights(floor_z.astype(jnp.int32), coord_z - floor_z, z_start, z_len)
    weight_y = axis_weights(floor_y.astype(jnp.int32), coord_y - floor_y, y_start, y_len)
    full = weight_z[:, :, None, :] * weight_y[:, None, :, :]
    full = full.reshape(orient_ids.shape[0], z_len * y_len, length)
    high = full.astype(jnp.bfloat16)
    low = (full - high.astype(jnp.float32)).astype(jnp.bfloat16)
    return (high, low)


def extract(planes, orient_ids, z_start, z_len, length):
    high, low = slice_matrix(orient_ids, length, z_start, z_len, 0, length)
    result = jnp.einsum("krj,rm->kjm", high, planes, preferred_element_type=jnp.float32)
    result = result + jnp.einsum("krj,rm->kjm", low, planes, preferred_element_type=jnp.float32)
    return result.reshape(orient_ids.shape[0], length, 2, length)


def backproject(slice_grads, orient_ids, z_start, z_len, y_start, y_len):
    length = slice_grads.shape[-1]
    count = slice_grads.shape[0]
    high, low = slice_matrix(orient_ids, length, z_start, z_len, y_start, y_len)
    flat = slice_grads.reshape(count, length, 2 * length)
    added = jnp.einsum("krj,kjm->rm", high, flat, preferred_element_type=jnp.float32)
    added = added + jnp.einsum("krj,kjm->rm", low, flat, preferred_element_type=jnp.float32)
    return added.reshape(z_len * y_len, 2, length)


def contrast(classes, length):
    offset = (jnp.arange(length, dtype=jnp.int32) - length // 2).astype(jnp.float32)
    radius = (offset[:, None] ** 2 + offset[None, :] ** 2) / (length * length)
    defocus = 30.0 + 10.0 * classes.astype(jnp.float32)
    return -jnp.sin(defocus[:, None, None] * radius[None] + 0.1)


def spectra(images):
    count = images.shape[0]
    length = images.shape[-1]
    freq_idx = jnp.arange(length, dtype=jnp.int32) - length // 2
    sample = jnp.arange(length, dtype=jnp.int32)
    phase_idx = freq_idx[:, None] * sample[None, :] % length
    dft_angle = -2.0 * jnp.pi / length * phase_idx.astype(jnp.float32)
    norm_factor = 1.0 / math.sqrt(length)
    basis_re = jnp.cos(dft_angle) * norm_factor
    basis_im = jnp.sin(dft_angle) * norm_factor
    stacked = jnp.stack([basis_re, basis_im], axis=0)
    stacked_hi = stacked.astype(jnp.bfloat16)
    stacked_lo = (stacked - stacked_hi.astype(jnp.float32)).astype(jnp.bfloat16)
    half = jnp.einsum("cjm,pmn->pjcn", stacked_hi, images, preferred_element_type=jnp.float32)
    half = half + jnp.einsum(
        "cjm,pmn->pjcn", stacked_lo, images, preferred_element_type=jnp.float32
    )
    trans_re = basis_re.T
    trans_im = basis_im.T
    complex_mat = jnp.concatenate(
        [
            jnp.concatenate([trans_re, trans_im], axis=1),
            jnp.concatenate([-trans_im, trans_re], axis=1),
        ],
        axis=0,
    )
    flat = half.reshape(count * length, 2 * length)
    result = jnp.dot(
        flat, complex_mat, precision=lax.Precision.HIGH, preferred_element_type=jnp.float32
    )
    return result.reshape(count, length, 2, length)


def per_device(volume, images, orientation, batch_slot, ctf_class):
    length = volume.shape[-1]
    slab_len = volume.shape[0]
    strip_len = length // lax.axis_size("dp")
    slab_start = lax.axis_index("group") * slab_len
    strip_start = lax.axis_index("dp") * strip_len
    own_orient = lax.dynamic_slice_in_dim(orientation, lax.axis_index("dp") * ORI_DEV, ORI_DEV)
    planes = volume.reshape(slab_len * length, 2 * length)
    partial_value = extract(planes, own_orient, slab_start, slab_len, length)
    slices = lax.psum(partial_value, "group")
    spectrum = spectra(images)
    factor = contrast(ctf_class, length)[:, :, None, :]
    predicted = jnp.take(slices, batch_slot, axis=0)
    residual = factor * predicted - spectrum
    weighted = factor * residual
    onehot = (batch_slot[:, None] == jnp.arange(ORI_DEV, dtype=jnp.int32)[None, :]).astype(
        jnp.float32
    )
    local_grads = jnp.einsum("ps,pjcx->sjcx", onehot, weighted, precision=lax.Precision.HIGHEST)
    slice_grads = lax.psum(local_grads, "group").astype(jnp.bfloat16)
    all_grads = lax.all_gather(slice_grads, "dp", axis=0, tiled=True)
    strip = backproject(all_grads, orientation, slab_start, slab_len, strip_start, strip_len)
    strip = strip.reshape(slab_len, strip_len, 2, length)
    prior_part = lax.dynamic_slice_in_dim(volume, strip_start, strip_len, 1).astype(jnp.float32)
    return strip + PRIOR_WEIGHT * prior_part


def solution(mesh):
    in_specs = (
        P("group", None, None, None),
        P(("dp", "group"), None, None),
        P(),
        P(("dp", "group")),
        P(("dp", "group")),
    )
    out_specs = P("group", "dp", None, None)
    return jax.shard_map(
        per_device, mesh=mesh, in_specs=in_specs, out_specs=out_specs, check_vma=False
    )
```

```python
import math

import jax
import jax.numpy as jnp
from jax import lax
from jax.sharding import PartitionSpec as P

NROT = 360
ORI_DEV = 2


PRIOR_WEIGHT = 0.25


def axis_weights(base, frac, start, span):
    cells = jnp.arange(span, dtype=jnp.int32) + start
    lower = (cells[None, :, None] == base[:, None, :]).astype(jnp.float32) * (1.0 - frac)[
        :, None, :
    ]
    upper = (cells[None, :, None] == (base + 1)[:, None, :]).astype(jnp.float32) * frac[:, None, :]
    return lower + upper


def slice_matrix(orient_ids, length, z_start, z_len, y_start, y_len):
    tilt_angle = jnp.pi * (orient_ids.astype(jnp.float32) + 0.5) / NROT
    offset = (jnp.arange(length, dtype=jnp.int32) - length // 2).astype(jnp.float32)
    coord_z = length / 2 + offset[None, :] * jnp.sin(tilt_angle)[:, None]
    coord_y = length / 2 + offset[None, :] * jnp.cos(tilt_angle)[:, None]
    floor_z = jnp.floor(coord_z)
    floor_y = jnp.floor(coord_y)
    weight_z = axis_weights(floor_z.astype(jnp.int32), coord_z - floor_z, z_start, z_len)
    weight_y = axis_weights(floor_y.astype(jnp.int32), coord_y - floor_y, y_start, y_len)
    full = weight_z[:, :, None, :] * weight_y[:, None, :, :]
    full = full.reshape(orient_ids.shape[0], z_len * y_len, length)
    high = full.astype(jnp.bfloat16)
    low = (full - high.astype(jnp.float32)).astype(jnp.bfloat16)
    return (high, low)


def extract(planes, orient_ids, z_start, z_len, length):
    high, low = slice_matrix(orient_ids, length, z_start, z_len, 0, length)
    result = jnp.einsum("krj,rm->kjm", high, planes, preferred_element_type=jnp.float32)
    result = result + jnp.einsum("krj,rm->kjm", low, planes, preferred_element_type=jnp.float32)
    return result.reshape(orient_ids.shape[0], length, 2, length)


def backproject(slice_grads, orient_ids, z_start, z_len, y_start, y_len):
    length = slice_grads.shape[-1]
    count = slice_grads.shape[0]
    high, low = slice_matrix(orient_ids, length, z_start, z_len, y_start, y_len)
    flat = slice_grads.reshape(count, length, 2 * length)
    added = jnp.einsum("krj,kjm->rm", high, flat, preferred_element_type=jnp.float32)
    added = added + jnp.einsum("krj,kjm->rm", low, flat, preferred_element_type=jnp.float32)
    return added.reshape(z_len * y_len, 2, length)


def contrast(classes, length):
    offset = (jnp.arange(length, dtype=jnp.int32) - length // 2).astype(jnp.float32)
    radius = (offset[:, None] ** 2 + offset[None, :] ** 2) / (length * length)
    defocus = 30.0 + 10.0 * classes.astype(jnp.float32)
    return -jnp.sin(defocus[:, None, None] * radius[None] + 0.1)


def spectra(images):
    count = images.shape[0]
    length = images.shape[-1]
    freq_idx = jnp.arange(length, dtype=jnp.int32) - length // 2
    sample = jnp.arange(length, dtype=jnp.int32)
    phase_idx = freq_idx[:, None] * sample[None, :] % length
    dft_angle = -2.0 * jnp.pi / length * phase_idx.astype(jnp.float32)
    norm_factor = 1.0 / math.sqrt(length)
    basis_re = jnp.cos(dft_angle) * norm_factor
    basis_im = jnp.sin(dft_angle) * norm_factor
    stacked = jnp.stack([basis_re, basis_im], axis=0)
    stacked_hi = stacked.astype(jnp.bfloat16)
    stacked_lo = (stacked - stacked_hi.astype(jnp.float32)).astype(jnp.bfloat16)
    half = jnp.einsum("cjm,pmn->pjcn", stacked_hi, images, preferred_element_type=jnp.float32)
    half = half + jnp.einsum(
        "cjm,pmn->pjcn", stacked_lo, images, preferred_element_type=jnp.float32
    )
    trans_re = basis_re.T
    trans_im = basis_im.T
    complex_mat = jnp.concatenate(
        [
            jnp.concatenate([trans_re, trans_im], axis=1),
            jnp.concatenate([-trans_im, trans_re], axis=1),
        ],
        axis=0,
    )
    flat = half.reshape(count * length, 2 * length)
    result = jnp.dot(
        flat, complex_mat, precision=lax.Precision.HIGH, preferred_element_type=jnp.float32
    )
    return result.reshape(count, length, 2, length)


def per_device(volume, images, orientation, batch_slot, ctf_class):
    length = volume.shape[-1]
    slab_len = volume.shape[0]
    strip_len = length // lax.axis_size("dp")
    slab_start = lax.axis_index("group") * slab_len
    strip_start = lax.axis_index("dp") * strip_len
    own_orient = lax.dynamic_slice_in_dim(orientation, lax.axis_index("dp") * ORI_DEV, ORI_DEV)
    planes = volume.reshape(slab_len * length, 2 * length)
    partial_value = extract(planes, own_orient, slab_start, slab_len, length)
    slices = lax.psum(partial_value, "group")
    spectrum = spectra(images)
    factor = contrast(ctf_class, length)[:, :, None, :]
    predicted = jnp.take(slices, batch_slot, axis=0)
    residual = factor * predicted - spectrum
    weighted = factor * residual
    onehot = (batch_slot[:, None] == jnp.arange(ORI_DEV, dtype=jnp.int32)[None, :]).astype(
        jnp.float32
    )
    local_grads = jnp.einsum("ps,pjcx->sjcx", onehot, weighted, precision=lax.Precision.HIGHEST)
    groups = lax.axis_size("group")
    dps = lax.axis_size("dp")
    part = lax.psum_scatter(local_grads, "group", scatter_dimension=1, tiled=True)
    part = part.astype(jnp.bfloat16)
    gathered = lax.all_gather(part, ("dp", "group"), axis=0, tiled=False)
    gathered = gathered.reshape(dps, groups, ORI_DEV, length // groups, 2, length)
    all_grads = gathered.transpose(0, 2, 1, 3, 4, 5).reshape(dps * ORI_DEV, length, 2, length)
    strip = backproject(all_grads, orientation, slab_start, slab_len, strip_start, strip_len)
    strip = strip.reshape(slab_len, strip_len, 2, length)
    prior_part = lax.dynamic_slice_in_dim(volume, strip_start, strip_len, 1).astype(jnp.float32)
    return strip + PRIOR_WEIGHT * prior_part


def solution(mesh):
    in_specs = (
        P("group", None, None, None),
        P(("dp", "group"), None, None),
        P(),
        P(("dp", "group")),
        P(("dp", "group")),
    )
    out_specs = P("group", "dp", None, None)
    return jax.shard_map(
        per_device, mesh=mesh, in_specs=in_specs, out_specs=out_specs, check_vma=False
    )
```

```python
import math

import jax
import jax.numpy as jnp
from jax import lax
from jax.sharding import PartitionSpec as P

NROT = 360
ORI_DEV = 2


PRIOR_WEIGHT = 0.25


def axis_weights(base, frac, start, span):
    cells = jnp.arange(span, dtype=jnp.int32) + start
    lower = (cells[None, :, None] == base[:, None, :]).astype(jnp.float32) * (1.0 - frac)[
        :, None, :
    ]
    upper = (cells[None, :, None] == (base + 1)[:, None, :]).astype(jnp.float32) * frac[:, None, :]
    return lower + upper


def slice_matrix(orient_ids, length, z_start, z_len, y_start, y_len):
    tilt_angle = jnp.pi * (orient_ids.astype(jnp.float32) + 0.5) / NROT
    offset = (jnp.arange(length, dtype=jnp.int32) - length // 2).astype(jnp.float32)
    coord_z = length / 2 + offset[None, :] * jnp.sin(tilt_angle)[:, None]
    coord_y = length / 2 + offset[None, :] * jnp.cos(tilt_angle)[:, None]
    floor_z = jnp.floor(coord_z)
    floor_y = jnp.floor(coord_y)
    weight_z = axis_weights(floor_z.astype(jnp.int32), coord_z - floor_z, z_start, z_len)
    weight_y = axis_weights(floor_y.astype(jnp.int32), coord_y - floor_y, y_start, y_len)
    full = weight_z[:, :, None, :] * weight_y[:, None, :, :]
    full = full.reshape(orient_ids.shape[0], z_len * y_len, length)
    high = full.astype(jnp.bfloat16)
    low = (full - high.astype(jnp.float32)).astype(jnp.bfloat16)
    return (high, low)


def extract(planes, orient_ids, z_start, z_len, length):
    high, low = slice_matrix(orient_ids, length, z_start, z_len, 0, length)
    result = jnp.einsum("krj,rm->kjm", high, planes, preferred_element_type=jnp.float32)
    result = result + jnp.einsum("krj,rm->kjm", low, planes, preferred_element_type=jnp.float32)
    return result.reshape(orient_ids.shape[0], length, 2, length)


def backproject(slice_grads, orient_ids, z_start, z_len, y_start, y_len):
    length = slice_grads.shape[-1]
    count = slice_grads.shape[0]
    high, low = slice_matrix(orient_ids, length, z_start, z_len, y_start, y_len)
    flat = slice_grads.reshape(count, length, 2 * length)
    added = jnp.einsum("krj,kjm->rm", high, flat, preferred_element_type=jnp.float32)
    added = added + jnp.einsum("krj,kjm->rm", low, flat, preferred_element_type=jnp.float32)
    return added.reshape(z_len * y_len, 2, length)


def contrast(classes, length):
    offset = (jnp.arange(length, dtype=jnp.int32) - length // 2).astype(jnp.float32)
    radius = (offset[:, None] ** 2 + offset[None, :] ** 2) / (length * length)
    defocus = 30.0 + 10.0 * classes.astype(jnp.float32)
    return -jnp.sin(defocus[:, None, None] * radius[None] + 0.1)


def spectra(images):
    count = images.shape[0]
    length = images.shape[-1]
    freq_idx = jnp.arange(length, dtype=jnp.int32) - length // 2
    sample = jnp.arange(length, dtype=jnp.int32)
    phase_idx = freq_idx[:, None] * sample[None, :] % length
    dft_angle = -2.0 * jnp.pi / length * phase_idx.astype(jnp.float32)
    norm_factor = 1.0 / math.sqrt(length)
    basis_re = jnp.cos(dft_angle) * norm_factor
    basis_im = jnp.sin(dft_angle) * norm_factor
    stacked = jnp.stack([basis_re, basis_im], axis=0)
    stacked_hi = stacked.astype(jnp.bfloat16)
    stacked_lo = (stacked - stacked_hi.astype(jnp.float32)).astype(jnp.bfloat16)
    half = jnp.einsum("cjm,pmn->pjcn", stacked_hi, images, preferred_element_type=jnp.float32)
    half = half + jnp.einsum(
        "cjm,pmn->pjcn", stacked_lo, images, preferred_element_type=jnp.float32
    )
    trans_re = basis_re.T
    trans_im = basis_im.T
    complex_mat = jnp.concatenate(
        [
            jnp.concatenate([trans_re, trans_im], axis=1),
            jnp.concatenate([-trans_im, trans_re], axis=1),
        ],
        axis=0,
    )
    flat = half.reshape(count * length, 2 * length)
    result = jnp.dot(
        flat, complex_mat, precision=lax.Precision.HIGH, preferred_element_type=jnp.float32
    )
    return result.reshape(count, length, 2, length)


def per_device(volume, images, orientation, batch_slot, ctf_class):
    length = volume.shape[-1]
    slab_len = volume.shape[0]
    strip_len = length // lax.axis_size("dp")
    slab_start = lax.axis_index("group") * slab_len
    strip_start = lax.axis_index("dp") * strip_len
    own_orient = lax.dynamic_slice_in_dim(orientation, lax.axis_index("dp") * ORI_DEV, ORI_DEV)
    planes = volume.reshape(slab_len * length, 2 * length)
    partial_value = extract(planes, own_orient, slab_start, slab_len, length)
    slices = lax.psum(partial_value, "group")
    spectrum = spectra(images)
    factor = contrast(ctf_class, length)[:, :, None, :]
    predicted = jnp.take(slices, batch_slot, axis=0)
    residual = factor * predicted - spectrum
    weighted = factor * residual
    onehot = (batch_slot[:, None] == jnp.arange(ORI_DEV, dtype=jnp.int32)[None, :]).astype(
        jnp.float32
    )
    local_grads = jnp.sum(onehot[:, :, None, None, None] * weighted[:, None], axis=0)
    slice_grads = lax.psum(local_grads, "group").astype(jnp.bfloat16)
    all_grads = lax.all_gather(slice_grads, "dp", axis=0, tiled=True)
    strip = backproject(all_grads, orientation, slab_start, slab_len, strip_start, strip_len)
    strip = strip.reshape(slab_len, strip_len, 2, length)
    prior_part = lax.dynamic_slice_in_dim(volume, strip_start, strip_len, 1).astype(jnp.float32)
    return strip + PRIOR_WEIGHT * prior_part


def solution(mesh):
    in_specs = (
        P("group", None, None, None),
        P(("dp", "group"), None, None),
        P(),
        P(("dp", "group")),
        P(("dp", "group")),
    )
    out_specs = P("group", "dp", None, None)
    return jax.shard_map(
        per_device, mesh=mesh, in_specs=in_specs, out_specs=out_specs, check_vma=False
    )
```
